32 devices in a mesh: shots: 2 (over y), depth: 4 (over x, core), freq: 4 (over z).
Axes of the slice: x: 2, y: 2, z: 4, core: 2. Of those that a mesh axis runs over, the one named last changes fastest.
Arguments:
- surface: bfloat16 [4, 4, 2, 384, 384], P('shots', 'freq'), parts along dimension 0, may hold values from -6 to 6
- kernels: bfloat16 [4, 4, 2, 25, 25], P('depth', 'freq'), may hold values from -0.15625 to 0.15625
- slowness: float32 [4, 384, 384], P('depth'), may hold values from -0.02 to 0.02
- freq_index: int32 [4], P('freq'), may hold values from 8 to 199
Outputs:
- image: float32 [8, 384, 384], P(('shots', 'depth'), 'freq'), parts along dimension 0
The draws below stay inside these ranges and needn't reach their ends.
There are 2 independent parts, one for each index of `shots`. The reference program is written for one: setup_inputs(seed, part) draws one part's arguments, and reference() takes and returns one part's arrays. A program takes and returns all parts, laid end to end along the dimension named above; an argument that names none is the same for every part. Nothing has to cross between parts.
All inputs are finite; a program needn't handle non-finite values.
Results may differ from the reference program's by a relative error of at most 0.0067.
Values may be sent and summed in bfloat16 or wider, within the bound.
A program may use at most 64 MiB of HBM per device.

```python
import math
import jax
import jax.numpy as jnp
from jax import lax

LX = 384
LY = 384
KW = 25
NF = 4
NZ = 4


def touch_ends(entries, rng, low, largest):
    spot = [jax.random.randint(jax.random.fold_in(rng, axis), (), 0, length) for axis, length in enumerate(entries.shape)]
    longest = entries.shape.index(max(entries.shape))
    beside = spot[:longest] + [(spot[longest] + 1) % entries.shape[longest]] + spot[longest + 1:]
    return entries.at[tuple(spot)].set(low).at[tuple(beside)].set(largest)


def steps_of(key, dims, shards, low, top_value):
    def one(position, parts):
        heights = jax.random.uniform(jax.random.fold_in(jax.random.fold_in(key, 6), position), (parts,), jnp.float32, low / len(shards), top_value / len(shards))
        return jnp.repeat(jnp.exp(heights), dims[position] // parts).reshape((-1,) + (1,) * (len(dims) - position - 1))

    factor_of = one(*shards[0])
    for cut in shards[1:]:
        factor_of = factor_of * one(*cut)
    return factor_of


def gaussian(own_key, shape, deviation, reach, shards=(), dtype=jnp.bfloat16):
    array = deviation * jax.random.normal(own_key, shape, jnp.float32)
    if shards:
        array = array * steps_of(own_key, shape, shards, -0.22, 0.18)
    return jnp.clip(array, -reach, reach).astype(dtype)


def setup_inputs(seed: int = 0, part: int = 0) -> dict:
    keys = jax.random.split(jax.random.key(seed), 5)
    part_keys = jax.random.split(jax.random.fold_in(keys[4], part), 5)
    surface = gaussian(part_keys[0], (2, NF, 2, LX, LY), 1.0, 6.0, ((1, 4),))
    kernels = gaussian(keys[1], (NZ, NF, 2, KW, KW), (2 * KW * KW) ** -0.5, 0.15625, ((0, 4), (1, 4)))
    slowness = jnp.clip(jax.random.uniform(keys[2], (NZ, LX, LY), jnp.float32, -0.02, 0.02) * steps_of(keys[2], (NZ, LX, LY), ((0, 4),), -0.4, 0.0), -0.02, 0.02)
    freq_index = touch_ends(jax.random.randint(keys[3], (NF,), 8, 200), jax.random.fold_in(keys[3], 1), 8, 199).astype(jnp.int32)
    return {"surface": surface, "kernels": kernels, "slowness": slowness, "freq_index": freq_index}


def extrapolate(wavefield, stencil, phase_rate, freq_bins):
    freq_count = wavefield.shape[1]
    cells_x = wavefield.shape[3]
    cells_y = wavefield.shape[4]
    tap_count = stencil.shape[-1]
    stacked = wavefield.reshape(2, freq_count * 2, cells_x, cells_y)
    real_part = stencil[:, 0]
    imag_part = stencil[:, 1]
    filters = jnp.stack([jnp.stack([real_part, -imag_part], 1), jnp.stack([imag_part, real_part], 1)], 1)
    filters = filters.reshape(freq_count * 2, 2, tap_count, tap_count)
    convolved = lax.conv_general_dilated(stacked, filters, (1, 1), 'SAME', dimension_numbers=('NCHW', 'OIHW', 'NCHW'), feature_group_count=freq_count, preferred_element_type=jnp.float32)
    convolved = convolved.reshape(2, freq_count, 2, cells_x, cells_y)
    phases = freq_bins.astype(jnp.float32)[:, None, None] * phase_rate[None]
    cosines = jnp.cos(phases)
    sine_terms = jnp.sin(phases)
    real_out = convolved[:, :, 0] * cosines - convolved[:, :, 1] * sine_terms
    imag_out = convolved[:, :, 0] * sine_terms + convolved[:, :, 1] * cosines
    stepped = jnp.stack([real_out, imag_out], 2).astype(jnp.bfloat16)
    widened = stepped.astype(jnp.float32)
    partial_sum = lax.optimization_barrier(jnp.sum(widened[0, :, 0] * widened[1, :, 0] + widened[0, :, 1] * widened[1, :, 1], axis=0))
    return (stepped, partial_sum)

def reference(surface, kernels, slowness, freq_index):

    def advance(wavefield, operands):
        stencil, phase_rate = operands
        stepped, partial_sum = extrapolate(wavefield, stencil, phase_rate, freq_index)
        return (stepped, partial_sum)
    final_wave, partials = lax.scan(advance, surface, (kernels, slowness))
    return partials * (1.0 / math.sqrt(NF))
```

```python
import functools
import math

import jax
import jax.numpy as jnp
from jax import lax
from jax.experimental import pallas as pl
from jax.experimental.pallas import tpu as pltpu
from jax.sharding import PartitionSpec as P


def with_halo(shard, sides, width):
    for axis, dim in sides:
        size, length = (lax.axis_size(axis), shard.shape[dim])
        up = [(i, (i + 1) % size) for i in range(size - 1)]
        down = [(j, i) for i, j in up]
        last = lax.slice_in_dim(shard, length - width, length, axis=dim)
        leading = lax.slice_in_dim(shard, 0, width, axis=dim)
        before = lax.ppermute(last, axis, up)
        after = lax.ppermute(leading, axis, down)
        shard = jnp.concatenate([before, shard, after], axis=dim)
    return shard


def convolve(padded, stencil, margin):
    rows_in = padded.shape[3]
    cells_y = padded.shape[4]
    tap_count = stencil.shape[-1]
    rows_out = rows_in - 2 * margin
    real_part = stencil[:, 0].astype(jnp.float32)
    imag_part = stencil[:, 1].astype(jnp.float32)
    filters = jnp.stack(
        [jnp.stack([real_part, -imag_part], 1), jnp.stack([imag_part, real_part], 1)], 1
    )
    offsets = lax.iota(jnp.int32, rows_in)[None, :] - lax.iota(jnp.int32, rows_out)[:, None]
    select = (offsets[None] == lax.iota(jnp.int32, tap_count)[:, None, None]).astype(jnp.float32)
    banded = jnp.einsum("fdcab,axk->fdxbck", filters, select).astype(jnp.bfloat16)
    widened = jnp.pad(padded, ((0, 0), (0, 0), (0, 0), (0, 0), (margin, margin)))
    patches = jnp.stack(
        [widened[:, :, :, :, shift : shift + cells_y] for shift in range(tap_count)], 0
    )
    return jnp.einsum("bwfcky,fdxbck->wfdxy", patches, banded, preferred_element_type=jnp.float32)


def rotate(convolved, phase_rate, freq_bins):
    phases = freq_bins[:, None, None] * phase_rate[None]
    cosines = jnp.cos(phases)
    sine_terms = jnp.sin(phases)
    real_out = convolved[:, :, 0] * cosines - convolved[:, :, 1] * sine_terms
    imag_out = convolved[:, :, 0] * sine_terms + convolved[:, :, 1] * cosines
    return jnp.stack([real_out, imag_out], 2).astype(jnp.bfloat16)


def correlate(stepped):
    widened = stepped.astype(jnp.float32)
    return jnp.sum(
        widened[0, :, 0] * widened[1, :, 0] + widened[0, :, 1] * widened[1, :, 1], axis=0
    )


def on_device_general(surface, kernels, slowness, freq_index):
    depth_count = lax.axis_size("depth")
    position = lax.axis_index("depth")
    cells_x = surface.shape[3]
    row_count = cells_x // depth_count
    tap_count = kernels.shape[-1]
    margin = (tap_count - 1) // 2
    start_row = position * row_count
    wavefield = lax.dynamic_slice_in_dim(surface, start_row, row_count, 3)
    stencils = lax.all_gather(kernels, "depth", axis=0, tiled=True)
    phase_rates = lax.all_to_all(slowness, "depth", split_axis=1, concat_axis=0, tiled=True)
    freq_bins = freq_index.astype(jnp.float32)

    def advance(wave, operands):
        stencil, phase_rate = operands
        padded = with_halo(wave, (("depth", 3),), margin)
        stepped = rotate(convolve(padded, stencil, margin), phase_rate, freq_bins)
        return (stepped, correlate(stepped))

    final_wave, partials = lax.scan(advance, wavefield, (stencils, phase_rates))
    moved = lax.all_to_all(partials, "depth", split_axis=0, concat_axis=1, tiled=True)
    summed = lax.psum_scatter(moved, "freq", scatter_dimension=1, tiled=True)
    return summed * (1.0 / math.sqrt(surface.shape[1] * lax.axis_size("freq")))


MESH = pl.DeviceIdType.MESH
VMEM = pl.BlockSpec(memory_space=pltpu.VMEM)
SCALE = 32767.0 / 0.02


def window(position, rows, cells, margin):
    length = min(cells, rows + 2 * margin)
    start = jnp.clip(position * rows - margin, 0, cells - length)
    offset = start - position * rows + 2 * margin
    return pl.multiple_of(start, 16), pl.multiple_of(offset, 16), length


def gather_kernel(depth_count, rows, margin, slow_ref, taps_ref, slow_out, taps_out, send, recv, local):
    me = lax.axis_index("depth")
    cells = slow_ref.shape[0]
    barrier = pltpu.get_barrier_semaphore()
    for step in range(1, depth_count):
        other = lax.rem(me + step, depth_count)
        pl.semaphore_signal(barrier, inc=1, device_id={"depth": other}, device_id_type=MESH)
    pl.semaphore_wait(barrier, depth_count - 1)
    copies = []
    for step in range(1, depth_count):
        other = lax.rem(me + step, depth_count)
        start, offset, length = window(other, rows, cells, margin)
        copies.append(pltpu.make_async_remote_copy(
            src_ref=taps_ref, dst_ref=taps_out.at[me],
            send_sem=send.at[0, step - 1], recv_sem=recv.at[0, step - 1],
            device_id={"depth": other}, device_id_type=MESH))
        copies.append(pltpu.make_async_remote_copy(
            src_ref=slow_ref.at[pl.ds(start, length)],
            dst_ref=slow_out.at[me, pl.ds(offset, length)],
            send_sem=send.at[1, step - 1], recv_sem=recv.at[1, step - 1],
            device_id={"depth": other}, device_id_type=MESH))
    for copy in copies:
        copy.start()
    start, offset, length = window(me, rows, cells, margin)
    own = [
        pltpu.make_async_copy(taps_ref, taps_out.at[me], local.at[0]),
        pltpu.make_async_copy(slow_ref.at[pl.ds(start, length)], slow_out.at[me, pl.ds(offset, length)], local.at[1]),
    ]
    for copy in own:
        copy.start()
    for copy in own + copies:
        copy.wait()


def gather(slow, taps, depth_count, rows, margin):
    frame = rows + 4 * margin
    return pl.pallas_call(
        functools.partial(gather_kernel, depth_count, rows, margin),
        out_shape=(
            jax.ShapeDtypeStruct((depth_count, frame, slow.shape[1]), slow.dtype),
            jax.ShapeDtypeStruct((depth_count,) + taps.shape, taps.dtype),
        ),
        in_specs=[VMEM] * 2,
        out_specs=(VMEM, VMEM),
        scratch_shapes=[
            pltpu.SemaphoreType.DMA((2, depth_count - 1)),
            pltpu.SemaphoreType.DMA((2, depth_count - 1)),
            pltpu.SemaphoreType.DMA((2,)),
        ],
        compiler_params=pltpu.CompilerParams(collective_id=0, has_side_effects=True),
    )(slow, taps)


def sine_cosine(phase):
    quarter = phase * 0.25
    sq = quarter * quarter
    sine = quarter * (1.0 + sq * (-1 / 6 + sq * (1 / 120 + sq * (-1 / 5040 + sq * (1 / 362880 - sq * (1 / 39916800))))))
    cosine = 1.0 + sq * (-0.5 + sq * (1 / 24 + sq * (-1 / 720 + sq * (1 / 40320 - sq * (1 / 3628800)))))
    for _ in range(2):
        sine, cosine = 2.0 * sine * cosine, 1.0 - 2.0 * sine * sine
    return sine, cosine


def tiles_of(total):
    if total <= 96:
        return [(0, total)]
    first = total // 2 // 16 * 16
    return [(0, first), (first, -(-(total - first) // 16) * 16)]


def march_kernel(depth_count, rows, reach, factor, freq_ref, surface_ref, slow_ref, taps_ref, image_ref,
                 wave0, wave1, band, patches, conv_ref, corr, sems):
    me = lax.axis_index("depth")
    margin = depth_count * reach
    cells = surface_ref.shape[3]
    cols = surface_ref.shape[4]
    width = 2 * reach + 1
    waves = (wave0, wave1)
    start, offset, length = window(me, rows, cells, margin)
    wave0[...] = jnp.zeros_like(wave0)
    wave1[...] = jnp.zeros_like(wave1)
    copies = [
        pltpu.make_async_copy(
            surface_ref.at[w, 0, c, pl.ds(start, length)],
            wave0.at[w, c, pl.ds(offset, length), pl.ds(128, cols)],
            sems.at[w, c])
        for w in range(2) for c in range(2)
    ]
    for copy in copies:
        copy.start()
    for copy in copies:
        copy.wait()
    freq = freq_ref[0].astype(jnp.float32) * (1.0 / SCALE)
    for z in range(depth_count):
        tap = taps_ref[z].astype(jnp.float32)

        @pl.loop(0, width)
        def _(b):
            parts = []
            for k in range(2):
                line = jnp.broadcast_to(taps_ref[z, pl.ds(32 * k + b, 1)], (112, 128))
                parts.append(pltpu.roll(line, 0, 1, stride=1, stride_axis=0))
            real, imag = parts
            low, high = pl.ds(pl.multiple_of(256 * b, 256), 128), pl.ds(pl.multiple_of(256 * b + 128, 128), 128)
            band[0, :, low] = real.astype(jnp.bfloat16)
            band[0, :, high] = (-imag).astype(jnp.bfloat16)
            band[1, :, low] = imag.astype(jnp.bfloat16)
            band[1, :, high] = real.astype(jnp.bfloat16)

        source, target = waves[z % 2], waves[(z + 1) % 2]
        base = margin if z == 0 else 0
        base_in = base
        shift = reach * (z + 1)
        total = rows + 2 * reach * (depth_count - 1 - z)
        for at, size in tiles_of(total):
            @pl.loop(0, 2)
            def _(c):
                for b in range(width):
                    for w in range(2):
                        patches[pl.ds(pl.multiple_of(256 * b + 128 * c, 128), 128), cols * w : cols * w + cols] = (
                            source[w, c, base_in + at : base_in + at + 128, 128 - reach + b : 128 - reach + b + cols])

            total_ref = conv_ref.at[pl.ds(0, 2 * size)]
            total_ref[...] = jnp.zeros((2 * size, 2 * cols), jnp.float32)

            @pl.loop(0, width // 5)
            def _(g):
                deep = pl.ds(pl.multiple_of(1280 * g, 1280), 1280)
                lhs = jnp.concatenate([band[0, :size, deep], band[1, :size, deep]], 0)
                total_ref[...] += jnp.dot(lhs, patches[deep, :], preferred_element_type=jnp.float32)

            conv = total_ref
            phase = slow_ref[z, margin + shift + at : margin + shift + at + size].astype(jnp.int32).astype(jnp.float32) * freq
            sine, cosine = sine_cosine(phase)
            line = lax.broadcasted_iota(jnp.int32, (size, cols), 0) + (me * rows - margin + shift + at)
            inside = (line >= 0) & (line < cells)
            kept = []
            for w in range(2):
                real = conv[:size, cols * w : cols * w + cols]
                imag = conv[size:, cols * w : cols * w + cols]
                for c, value in enumerate((real * cosine - imag * sine, real * sine + imag * cosine)):
                    value = jnp.where(inside, value, 0.0).astype(jnp.bfloat16)
                    kept.append(value.astype(jnp.float32))
                    if z + 1 < depth_count:
                        target[w, c, at : at + size, 128 : 128 + cols] = value
            corr[at : at + size] = (kept[0] * kept[2] + kept[1] * kept[3]) * factor
        image_ref[z] = corr[margin - shift : margin - shift + rows].astype(image_ref.dtype)


def march(freq, surface, slow, taps, depth_count, rows, reach, factor):
    cols = surface.shape[4]
    width = 2 * reach + 1
    frame = slow.shape[1]
    return pl.pallas_call(
        functools.partial(march_kernel, depth_count, rows, reach, factor),
        out_shape=jax.ShapeDtypeStruct((depth_count, rows, cols), jnp.bfloat16),
        in_specs=[pl.BlockSpec(memory_space=pltpu.SMEM), pl.BlockSpec(memory_space=pl.ANY), VMEM, VMEM],
        out_specs=VMEM,
        scratch_shapes=[
            pltpu.VMEM((2, 2, frame, cols + 256), jnp.bfloat16),
            pltpu.VMEM((2, 2, frame, cols + 256), jnp.bfloat16),
            pltpu.VMEM((2, 112, 256 * width), jnp.bfloat16),
            pltpu.VMEM((256 * width, 2 * cols), jnp.bfloat16),
            pltpu.VMEM((192, 2 * cols), jnp.float32),
            pltpu.VMEM((192, cols), jnp.float32),
            pltpu.SemaphoreType.DMA((2, 2)),
        ],
        compiler_params=pltpu.CompilerParams(vmem_limit_bytes=48 << 20),
    )(freq, surface, slow, taps)


def spread_kernel(count, image_ref, out_ref, slots, send, recv, local):
    depth = lax.axis_index("depth")
    freq = lax.axis_index("freq")
    barrier = pltpu.get_barrier_semaphore()
    for k in range(count):
        @pl.when((depth != freq) | (k != freq))
        def _():
            pl.semaphore_signal(barrier, inc=1, device_id={"depth": freq, "freq": k}, device_id_type=MESH)
    pl.semaphore_wait(barrier, count - (depth == freq).astype(jnp.int32))

    def outgoing(k):
        return pltpu.make_async_remote_copy(
            src_ref=image_ref.at[k], dst_ref=slots.at[freq],
            send_sem=send.at[k], recv_sem=recv.at[freq],
            device_id={"depth": k, "freq": depth}, device_id_type=MESH)

    def incoming(k):
        return pltpu.make_async_remote_copy(
            src_ref=image_ref.at[k], dst_ref=slots.at[k],
            send_sem=send.at[k], recv_sem=recv.at[k],
            device_id={"depth": k, "freq": depth}, device_id_type=MESH)

    for k in range(count):
        @pl.when((depth != freq) | (k != depth))
        def _():
            outgoing(k).start()

    own = pltpu.make_async_copy(image_ref.at[depth], slots.at[freq], local)

    @pl.when(depth == freq)
    def _():
        own.start()
        own.wait()

    for k in range(count):
        @pl.when((depth != freq) | (k != freq))
        def _():
            incoming(k).wait_recv()
    total = slots[0].astype(jnp.float32)
    for k in range(1, count):
        total = total + slots[k].astype(jnp.float32)
    out_ref[0] = total
    for k in range(count):
        @pl.when((depth != freq) | (k != depth))
        def _():
            outgoing(k).wait_send()


def spread(image):
    count = image.shape[0]
    return pl.pallas_call(
        functools.partial(spread_kernel, count),
        out_shape=jax.ShapeDtypeStruct((1,) + image.shape[1:], jnp.float32),
        in_specs=[VMEM],
        out_specs=VMEM,
        scratch_shapes=[
            pltpu.VMEM(image.shape, image.dtype),
            pltpu.SemaphoreType.DMA((count,)),
            pltpu.SemaphoreType.DMA((count,)),
            pltpu.SemaphoreType.DMA,
        ],
        compiler_params=pltpu.CompilerParams(collective_id=1, has_side_effects=True),
    )(image)


def on_device_fused(surface, kernels, slowness, freq_index):
    depth_count = lax.axis_size("depth")
    cells = surface.shape[3]
    rows = cells // depth_count
    width = kernels.shape[-1]
    reach = (width - 1) // 2
    margin = depth_count * reach
    taps = jnp.pad(jnp.swapaxes(kernels[0, 0], 1, 2), ((0, 0), (0, 32 - width), (0, 128 - width))).reshape(64, 128)
    slow = jnp.round(slowness[0] * SCALE).astype(jnp.int16)
    slow_all, taps_all = gather(slow, taps, depth_count, rows, margin)
    factor = 1.0 / math.sqrt(lax.axis_size("freq"))
    image = march(freq_index, surface, slow_all, taps_all.astype(jnp.float32), depth_count, rows, reach, factor)
    return spread(image)


def fits(mesh):
    return mesh.shape["depth"] == 4 and mesh.shape["freq"] == 4


def solution(mesh):
    in_specs = (
        P("shots", "freq", None, None, None),
        P("depth", "freq", None, None, None),
        P("depth", None, None),
        P("freq"),
    )
    out_specs = P(("shots", "depth"), "freq", None)
    body = on_device_fused if fits(mesh) else on_device_general
    return jax.shard_map(
        body, mesh=mesh, in_specs=in_specs, out_specs=out_specs, check_vma=False
    )
```

```python
import functools
import math

import jax
import jax.numpy as jnp
from jax import lax
from jax.experimental import pallas as pl
from jax.experimental.pallas import tpu as pltpu
from jax.sharding import PartitionSpec as P


def with_halo(shard, sides, width):
    for axis, dim in sides:
        size, length = (lax.axis_size(axis), shard.shape[dim])
        up = [(i, (i + 1) % size) for i in range(size - 1)]
        down = [(j, i) for i, j in up]
        last = lax.slice_in_dim(shard, length - width, length, axis=dim)
        leading = lax.slice_in_dim(shard, 0, width, axis=dim)
        before = lax.ppermute(last, axis, up)
        after = lax.ppermute(leading, axis, down)
        shard = jnp.concatenate([before, shard, after], axis=dim)
    return shard


def convolve(padded, stencil, margin):
    rows_in = padded.shape[3]
    cells_y = padded.shape[4]
    tap_count = stencil.shape[-1]
    rows_out = rows_in - 2 * margin
    real_part = stencil[:, 0].astype(jnp.float32)
    imag_part = stencil[:, 1].astype(jnp.float32)
    filters = jnp.stack(
        [jnp.stack([real_part, -imag_part], 1), jnp.stack([imag_part, real_part], 1)], 1
    )
    offsets = lax.iota(jnp.int32, rows_in)[None, :] - lax.iota(jnp.int32, rows_out)[:, None]
    select = (offsets[None] == lax.iota(jnp.int32, tap_count)[:, None, None]).astype(jnp.float32)
    banded = jnp.einsum("fdcab,axk->fdxbck", filters, select).astype(jnp.bfloat16)
    widened = jnp.pad(padded, ((0, 0), (0, 0), (0, 0), (0, 0), (margin, margin)))
    patches = jnp.stack(
        [widened[:, :, :, :, shift : shift + cells_y] for shift in range(tap_count)], 0
    )
    return jnp.einsum("bwfcky,fdxbck->wfdxy", patches, banded, preferred_element_type=jnp.float32)


def rotate(convolved, phase_rate, freq_bins):
    phases = freq_bins[:, None, None] * phase_rate[None]
    cosines = jnp.cos(phases)
    sine_terms = jnp.sin(phases)
    real_out = convolved[:, :, 0] * cosines - convolved[:, :, 1] * sine_terms
    imag_out = convolved[:, :, 0] * sine_terms + convolved[:, :, 1] * cosines
    return jnp.stack([real_out, imag_out], 2).astype(jnp.bfloat16)


def correlate(stepped):
    widened = stepped.astype(jnp.float32)
    return jnp.sum(
        widened[0, :, 0] * widened[1, :, 0] + widened[0, :, 1] * widened[1, :, 1], axis=0
    )


def on_device_general(surface, kernels, slowness, freq_index):
    depth_count = lax.axis_size("depth")
    position = lax.axis_index("depth")
    cells_x = surface.shape[3]
    row_count = cells_x // depth_count
    tap_count = kernels.shape[-1]
    margin = (tap_count - 1) // 2
    start_row = position * row_count
    wavefield = lax.dynamic_slice_in_dim(surface, start_row, row_count, 3)
    stencils = lax.all_gather(kernels, "depth", axis=0, tiled=True)
    phase_rates = lax.all_to_all(slowness, "depth", split_axis=1, concat_axis=0, tiled=True)
    freq_bins = freq_index.astype(jnp.float32)

    def advance(wave, operands):
        stencil, phase_rate = operands
        padded = with_halo(wave, (("depth", 3),), margin)
        stepped = rotate(convolve(padded, stencil, margin), phase_rate, freq_bins)
        return (stepped, correlate(stepped))

    final_wave, partials = lax.scan(advance, wavefield, (stencils, phase_rates))
    moved = lax.all_to_all(partials, "depth", split_axis=0, concat_axis=1, tiled=True)
    summed = lax.psum_scatter(moved, "freq", scatter_dimension=1, tiled=True)
    return summed * (1.0 / math.sqrt(surface.shape[1] * lax.axis_size("freq")))


MESH = pl.DeviceIdType.MESH
VMEM = pl.BlockSpec(memory_space=pltpu.VMEM)
SCALE = 32767.0 / 0.02


def window(position, rows, cells, margin):
    length = min(cells, rows + 2 * margin)
    start = jnp.clip(position * rows - margin, 0, cells - length)
    offset = start - position * rows + 2 * margin
    return pl.multiple_of(start, 16), pl.multiple_of(offset, 16), length


def sine_cosine(phase):
    quarter = phase * 0.25
    sq = quarter * quarter
    sine = quarter * (1.0 + sq * (-1 / 6 + sq * (1 / 120 + sq * (-1 / 5040 + sq * (1 / 362880 - sq * (1 / 39916800))))))
    cosine = 1.0 + sq * (-0.5 + sq * (1 / 24 + sq * (-1 / 720 + sq * (1 / 40320 - sq * (1 / 3628800)))))
    for _ in range(2):
        sine, cosine = 2.0 * sine * cosine, 1.0 - 2.0 * sine * sine
    return sine, cosine


def tiles_of(total):
    if total <= 96:
        return [(0, total)]
    first = total // 2 // 16 * 16
    return [(0, first), (first, -(-(total - first) // 16) * 16)]


def march_kernel(depth_count, rows, reach, factor, freq_ref, surface_ref, slow_ref, taps_ref, out_ref,
                 wave0, wave1, band, patches, conv_ref, corr, slow_all, taps_all, image, slots,
                 sems, local, send, recv, image_send, image_recv):
    me = lax.axis_index("depth")
    freq_at = lax.axis_index("freq")
    count = depth_count
    margin = depth_count * reach
    cells = surface_ref.shape[3]
    cols = surface_ref.shape[4]
    width = 2 * reach + 1
    waves = (wave0, wave1)

    barrier = pltpu.get_barrier_semaphore()
    for step in range(1, count):
        other = lax.rem(me + step, count)
        pl.semaphore_signal(barrier, inc=1, device_id={"depth": other}, device_id_type=MESH)
    for k in range(count):
        @pl.when((me != freq_at) | (k != freq_at))
        def _():
            pl.semaphore_signal(barrier, inc=1, device_id={"depth": freq_at, "freq": k}, device_id_type=MESH)
    pl.semaphore_wait(barrier, 2 * count - 1 - (me == freq_at).astype(jnp.int32))

    tap_copies = []
    slow_copies = []
    for step in range(1, count):
        other = lax.rem(me + step, count)
        start, offset, length = window(other, rows, cells, margin)
        tap_copies.append(pltpu.make_async_remote_copy(
            src_ref=taps_ref, dst_ref=taps_all.at[me],
            send_sem=send.at[0, step - 1], recv_sem=recv.at[0, step - 1],
            device_id={"depth": other}, device_id_type=MESH))
        slow_copies.append(pltpu.make_async_remote_copy(
            src_ref=slow_ref.at[pl.ds(start, length)],
            dst_ref=slow_all.at[me, pl.ds(offset, length)],
            send_sem=send.at[1, step - 1], recv_sem=recv.at[1, step - 1],
            device_id={"depth": other}, device_id_type=MESH))
    start, offset, length = window(me, rows, cells, margin)
    tap_copies.append(pltpu.make_async_copy(taps_ref, taps_all.at[me], local.at[0]))
    slow_copies.append(pltpu.make_async_copy(
        slow_ref.at[pl.ds(start, length)], slow_all.at[me, pl.ds(offset, length)], local.at[1]))
    for copy in tap_copies + slow_copies:
        copy.start()

    wave0[...] = jnp.zeros_like(wave0)
    copies = [
        pltpu.make_async_copy(
            surface_ref.at[w, 0, c, pl.ds(start, length)],
            wave0.at[w, c, pl.ds(offset, length), pl.ds(0, cols)],
            sems.at[w, c])
        for w in range(2) for c in range(2)
    ]
    for copy in copies:
        copy.start()
    wave1[:, :, :, cols:] = jnp.zeros(wave1.shape[:3] + (128,), wave1.dtype)
    top = rows + 2 * margin
    patches[:, top:] = jnp.zeros((2 * width, patches.shape[1] - top, 2 * cols), patches.dtype)
    for copy in copies:
        copy.wait()

    freq = freq_ref[0].astype(jnp.float32) * (1.0 / SCALE)

    def outgoing(z):
        return pltpu.make_async_remote_copy(
            src_ref=image.at[z], dst_ref=slots.at[freq_at],
            send_sem=image_send.at[z], recv_sem=image_recv.at[freq_at],
            device_id={"depth": z, "freq": me}, device_id_type=MESH)

    def incoming(k):
        return pltpu.make_async_remote_copy(
            src_ref=image.at[k], dst_ref=slots.at[k],
            send_sem=image_send.at[k], recv_sem=image_recv.at[k],
            device_id={"depth": k, "freq": me}, device_id_type=MESH)

    for z in range(count):
        source, target = waves[z % 2], waves[(z + 1) % 2]
        base = margin if z == 0 else 0
        shift = reach * (z + 1)
        total = rows + 2 * reach * (count - 1 - z)
        needed = -(-(total + 2 * reach) // 16) * 16

        @pl.loop(0, 2)
        def _(c):
            for w in range(2):
                for low in range(0, needed, 64):
                    size = min(64, needed - low)
                    block = source[w, c, base + low : base + low + size]
                    for b in range(width):
                        moved = pltpu.roll(block, (reach - b) % (cols + 128), 1)
                        patches[2 * b + c, low : low + size, cols * w : cols * w + cols] = moved[:, :cols]

        if z == 0:
            for copy in tap_copies:
                copy.wait()

        @pl.loop(0, width, unroll=5)
        def _(b):
            parts = []
            for k in range(2):
                line = jnp.broadcast_to(taps_all[z, pl.ds(32 * k + b, 1)], (112, 128))
                parts.append(pltpu.roll(line, 0, 1, stride=1, stride_axis=0))
            real, imag = parts
            low, high = pl.ds(pl.multiple_of(256 * b, 256), 128), pl.ds(pl.multiple_of(256 * b + 128, 128), 128)
            band[0, :, low] = real.astype(jnp.bfloat16)
            band[0, :, high] = (-imag).astype(jnp.bfloat16)
            band[1, :, low] = imag.astype(jnp.bfloat16)
            band[1, :, high] = real.astype(jnp.bfloat16)

        for at, size in tiles_of(total):
            total_ref = conv_ref.at[pl.ds(0, 2 * size)]
            total_ref[...] = jnp.zeros((2 * size, 2 * cols), jnp.float32)

            @pl.loop(0, width // 5)
            def _(g):
                deep = pl.ds(pl.multiple_of(1280 * g, 1280), 1280)
                lhs = jnp.concatenate([band[0, :size, deep], band[1, :size, deep]], 0)
                rhs = patches[pl.ds(10 * g, 10), at : at + 128].reshape(1280, 2 * cols)
                total_ref[...] += jnp.dot(lhs, rhs, preferred_element_type=jnp.float32)

            if z == 0 and at == 0:
                for copy in slow_copies:
                    copy.wait()
            phase = slow_all[z, margin + shift + at : margin + shift + at + size].astype(jnp.int32).astype(jnp.float32) * freq
            sine, cosine = sine_cosine(phase)
            line = lax.broadcasted_iota(jnp.int32, (size, cols), 0) + (me * rows - margin + shift + at)
            inside = (line >= 0) & (line < cells)
            kept = []
            for w in range(2):
                real = total_ref[:size, cols * w : cols * w + cols]
                imag = total_ref[size:, cols * w : cols * w + cols]
                for c, value in enumerate((real * cosine - imag * sine, real * sine + imag * cosine)):
                    value = jnp.where(inside, value, 0.0).astype(jnp.bfloat16)
                    kept.append(value.astype(jnp.float32))
                    if z + 1 < count:
                        target[w, c, at : at + size, :cols] = value
            corr[at : at + size] = (kept[0] * kept[2] + kept[1] * kept[3]) * factor
        image[z] = corr[margin - shift : margin - shift + rows].astype(image.dtype)

        @pl.when((me != freq_at) | (z != me))
        def _():
            outgoing(z).start()

    own = pltpu.make_async_copy(image.at[me], slots.at[freq_at], local.at[2])

    @pl.when(me == freq_at)
    def _():
        own.start()
        own.wait()

    for k in range(count):
        @pl.when((me != freq_at) | (k != freq_at))
        def _():
            incoming(k).wait_recv()
    result = slots[0].astype(jnp.float32)
    for k in range(1, count):
        result = result + slots[k].astype(jnp.float32)
    out_ref[0] = result
    for k in range(count):
        @pl.when((me != freq_at) | (k != me))
        def _():
            outgoing(k).wait_send()


def march(freq, surface, slow, taps, depth_count, rows, reach, factor):
    cols = surface.shape[4]
    width = 2 * reach + 1
    frame = rows + 4 * depth_count * reach
    peers = depth_count - 1
    return pl.pallas_call(
        functools.partial(march_kernel, depth_count, rows, reach, factor),
        out_shape=jax.ShapeDtypeStruct((1, rows, cols), jnp.float32),
        in_specs=[pl.BlockSpec(memory_space=pltpu.SMEM), pl.BlockSpec(memory_space=pl.ANY), VMEM, VMEM],
        out_specs=VMEM,
        scratch_shapes=[
            pltpu.VMEM((2, 2, frame, cols + 128), jnp.bfloat16),
            pltpu.VMEM((2, 2, frame, cols + 128), jnp.bfloat16),
            pltpu.VMEM((2, 112, 256 * width), jnp.bfloat16),
            pltpu.VMEM((2 * width, 208, 2 * cols), jnp.bfloat16),
            pltpu.VMEM((192, 2 * cols), jnp.float32),
            pltpu.VMEM((192, cols), jnp.float32),
            pltpu.VMEM((depth_count, frame, cols), slow.dtype),
            pltpu.VMEM((depth_count,) + taps.shape, taps.dtype),
            pltpu.VMEM((depth_count, rows, cols), jnp.bfloat16),
            pltpu.VMEM((depth_count, rows, cols), jnp.bfloat16),
            pltpu.SemaphoreType.DMA((2, 2)),
            pltpu.SemaphoreType.DMA((3,)),
            pltpu.SemaphoreType.DMA((2, peers)),
            pltpu.SemaphoreType.DMA((2, peers)),
            pltpu.SemaphoreType.DMA((depth_count,)),
            pltpu.SemaphoreType.DMA((depth_count,)),
        ],
        compiler_params=pltpu.CompilerParams(collective_id=0, has_side_effects=True, vmem_limit_bytes=48 << 20),
    )(freq, surface, slow, taps)


def on_device_fused(surface, kernels, slowness, freq_index):
    depth_count = lax.axis_size("depth")
    rows = surface.shape[3] // depth_count
    width = kernels.shape[-1]
    reach = (width - 1) // 2
    taps = jnp.pad(jnp.swapaxes(kernels[0, 0], 1, 2), ((0, 0), (0, 32 - width), (0, 128 - width)))
    taps = taps.reshape(64, 128).astype(jnp.float32)
    slow = jnp.round(slowness[0] * SCALE).astype(jnp.int16)
    factor = 1.0 / math.sqrt(lax.axis_size("freq"))
    return march(freq_index, surface, slow, taps, depth_count, rows, reach, factor)


def fits(mesh):
    return mesh.shape["depth"] == 4 and mesh.shape["freq"] == 4


def solution(mesh):
    in_specs = (
        P("shots", "freq", None, None, None),
        P("depth", "freq", None, None, None),
        P("depth", None, None),
        P("freq"),
    )
    out_specs = P(("shots", "depth"), "freq", None)
    body = on_device_fused if fits(mesh) else on_device_general
    return jax.shard_map(
        body, mesh=mesh, in_specs=in_specs, out_specs=out_specs, check_vma=False
    )
```

```python
import functools
import math

import jax
import jax.numpy as jnp
from jax import lax
from jax.experimental import pallas as pl
from jax.experimental.pallas import tpu as pltpu
from jax.sharding import PartitionSpec as P


def with_halo(shard, sides, width):
    for axis, dim in sides:
        size, length = (lax.axis_size(axis), shard.shape[dim])
        up = [(i, (i + 1) % size) for i in range(size - 1)]
        down = [(j, i) for i, j in up]
        last = lax.slice_in_dim(shard, length - width, length, axis=dim)
        leading = lax.slice_in_dim(shard, 0, width, axis=dim)
        before = lax.ppermute(last, axis, up)
        after = lax.ppermute(leading, axis, down)
        shard = jnp.concatenate([before, shard, after], axis=dim)
    return shard


def convolve(padded, stencil, margin):
    rows_in = padded.shape[3]
    cells_y = padded.shape[4]
    tap_count = stencil.shape[-1]
    rows_out = rows_in - 2 * margin
    real_part = stencil[:, 0].astype(jnp.float32)
    imag_part = stencil[:, 1].astype(jnp.float32)
    filters = jnp.stack(
        [jnp.stack([real_part, -imag_part], 1), jnp.stack([imag_part, real_part], 1)], 1
    )
    offsets = lax.iota(jnp.int32, rows_in)[None, :] - lax.iota(jnp.int32, rows_out)[:, None]
    select = (offsets[None] == lax.iota(jnp.int32, tap_count)[:, None, None]).astype(jnp.float32)
    banded = jnp.einsum("fdcab,axk->fdxbck", filters, select).astype(jnp.bfloat16)
    widened = jnp.pad(padded, ((0, 0), (0, 0), (0, 0), (0, 0), (margin, margin)))
    patches = jnp.stack(
        [widened[:, :, :, :, shift : shift + cells_y] for shift in range(tap_count)], 0
    )
    return jnp.einsum("bwfcky,fdxbck->wfdxy", patches, banded, preferred_element_type=jnp.float32)


def rotate(convolved, phase_rate, freq_bins):
    phases = freq_bins[:, None, None] * phase_rate[None]
    cosines = jnp.cos(phases)
    sine_terms = jnp.sin(phases)
    real_out = convolved[:, :, 0] * cosines - convolved[:, :, 1] * sine_terms
    imag_out = convolved[:, :, 0] * sine_terms + convolved[:, :, 1] * cosines
    return jnp.stack([real_out, imag_out], 2).astype(jnp.bfloat16)


def correlate(stepped):
    widened = stepped.astype(jnp.float32)
    return jnp.sum(
        widened[0, :, 0] * widened[1, :, 0] + widened[0, :, 1] * widened[1, :, 1], axis=0
    )


def on_device_general(surface, kernels, slowness, freq_index):
    depth_count = lax.axis_size("depth")
    position = lax.axis_index("depth")
    cells_x = surface.shape[3]
    row_count = cells_x // depth_count
    tap_count = kernels.shape[-1]
    margin = (tap_count - 1) // 2
    start_row = position * row_count
    wavefield = lax.dynamic_slice_in_dim(surface, start_row, row_count, 3)
    stencils = lax.all_gather(kernels, "depth", axis=0, tiled=True)
    phase_rates = lax.all_to_all(slowness, "depth", split_axis=1, concat_axis=0, tiled=True)
    freq_bins = freq_index.astype(jnp.float32)

    def advance(wave, operands):
        stencil, phase_rate = operands
        padded = with_halo(wave, (("depth", 3),), margin)
        stepped = rotate(convolve(padded, stencil, margin), phase_rate, freq_bins)
        return (stepped, correlate(stepped))

    final_wave, partials = lax.scan(advance, wavefield, (stencils, phase_rates))
    moved = lax.all_to_all(partials, "depth", split_axis=0, concat_axis=1, tiled=True)
    summed = lax.psum_scatter(moved, "freq", scatter_dimension=1, tiled=True)
    return summed * (1.0 / math.sqrt(surface.shape[1] * lax.axis_size("freq")))


MESH = pl.DeviceIdType.MESH
VMEM = pl.BlockSpec(memory_space=pltpu.VMEM)
SCALE = 32767.0 / 0.02


def window(position, rows, cells, margin):
    length = min(cells, rows + 2 * margin)
    start = jnp.clip(position * rows - margin, 0, cells - length)
    offset = start - position * rows + 2 * margin
    return pl.multiple_of(start, 16), pl.multiple_of(offset, 16), length


def sine_cosine(phase):
    quarter = phase * 0.25
    sq = quarter * quarter
    sine = quarter * (1.0 + sq * (-1 / 6 + sq * (1 / 120 + sq * (-1 / 5040 + sq * (1 / 362880 - sq * (1 / 39916800))))))
    cosine = 1.0 + sq * (-0.5 + sq * (1 / 24 + sq * (-1 / 720 + sq * (1 / 40320 - sq * (1 / 3628800)))))
    for _ in range(2):
        sine, cosine = 2.0 * sine * cosine, 1.0 - 2.0 * sine * sine
    return sine, cosine


def tiles_of(total):
    if total <= 96:
        return [(0, total)]
    first = total // 2 // 16 * 16
    return [(0, first), (first, -(-(total - first) // 16) * 16)]


def march_kernel(depth_count, rows, reach, factor, freq_ref, surface_ref, slow_ref, taps_ref, out_ref,
                 wave0, wave1, band, even, odd, conv_ref, corr, slow_all, taps_all, image, slots,
                 sems, local, send, recv, image_send, image_recv):
    me = lax.axis_index("depth")
    freq_at = lax.axis_index("freq")
    count = depth_count
    margin = depth_count * reach
    cells = surface_ref.shape[3]
    cols = surface_ref.shape[4]
    width = 2 * reach + 1
    waves = (wave0, wave1)
    patches = (even, odd)

    barrier = pltpu.get_barrier_semaphore()
    for step in range(1, count):
        other = lax.rem(me + step, count)
        pl.semaphore_signal(barrier, inc=1, device_id={"depth": other}, device_id_type=MESH)
    for k in range(count):
        @pl.when((me != freq_at) | (k != freq_at))
        def _():
            pl.semaphore_signal(barrier, inc=1, device_id={"depth": freq_at, "freq": k}, device_id_type=MESH)
    pl.semaphore_wait(barrier, 2 * count - 1 - (me == freq_at).astype(jnp.int32))

    tap_copies = []
    slow_copies = []
    for step in range(1, count):
        other = lax.rem(me + step, count)
        start, offset, length = window(other, rows, cells, margin)
        tap_copies.append(pltpu.make_async_remote_copy(
            src_ref=taps_ref, dst_ref=taps_all.at[me],
            send_sem=send.at[0, step - 1], recv_sem=recv.at[0, step - 1],
            device_id={"depth": other}, device_id_type=MESH))
        slow_copies.append(pltpu.make_async_remote_copy(
            src_ref=slow_ref.at[pl.ds(start, length)],
            dst_ref=slow_all.at[me, pl.ds(offset, length)],
            send_sem=send.at[1, step - 1], recv_sem=recv.at[1, step - 1],
            device_id={"depth": other}, device_id_type=MESH))
    start, offset, length = window(me, rows, cells, margin)
    tap_copies.append(pltpu.make_async_copy(taps_ref, taps_all.at[me], local.at[0]))
    slow_copies.append(pltpu.make_async_copy(
        slow_ref.at[pl.ds(start, length)], slow_all.at[me, pl.ds(offset, length)], local.at[1]))
    for copy in tap_copies + slow_copies:
        copy.start()

    wave0[...] = jnp.zeros_like(wave0)
    copies = [
        pltpu.make_async_copy(
            surface_ref.at[w, 0, c, pl.ds(start, length)],
            wave0.at[w, c, pl.ds(offset, length), pl.ds(0, cols)],
            sems.at[w, c])
        for w in range(2) for c in range(2)
    ]
    for copy in copies:
        copy.start()
    wave1[:, :, :, cols:] = jnp.zeros(wave1.shape[:3] + (128,), wave1.dtype)
    top = rows + 2 * margin
    for held in patches:
        held[:, top:] = jnp.zeros((10, held.shape[1] - top, 2 * cols), held.dtype)
    for copy in copies:
        copy.wait()

    freq = freq_ref[0].astype(jnp.float32) * (1.0 / SCALE)

    def outgoing(z):
        return pltpu.make_async_remote_copy(
            src_ref=image.at[z], dst_ref=slots.at[freq_at],
            send_sem=image_send.at[z], recv_sem=image_recv.at[freq_at],
            device_id={"depth": z, "freq": me}, device_id_type=MESH)

    def incoming(k):
        return pltpu.make_async_remote_copy(
            src_ref=image.at[k], dst_ref=slots.at[k],
            send_sem=image_send.at[k], recv_sem=image_recv.at[k],
            device_id={"depth": k, "freq": me}, device_id_type=MESH)

    for z in range(count):
        source, target = waves[z % 2], waves[(z + 1) % 2]
        base = margin if z == 0 else 0
        shift = reach * (z + 1)
        total = rows + 2 * reach * (count - 1 - z)
        needed = -(-(total + 2 * reach) // 16) * 16

        def build(group, chunk):
            held = patches[group % 2]
            c, w, low = chunk
            size = min(64, needed - low)
            block = source[w, c, base + low : base + low + size]
            for b in range(5):
                moved = pltpu.roll(block, (reach - 5 * group - b) % (cols + 128), 1)
                held[2 * b + c, low : low + size, cols * w : cols * w + cols] = moved[:, :cols]

        chunks = [(c, w, low) for c in range(2) for w in range(2) for low in range(0, needed, 64)]
        for chunk in chunks:
            build(0, chunk)

        if z == 0:
            for copy in tap_copies:
                copy.wait()

        @pl.loop(0, width, unroll=5)
        def _(b):
            parts = []
            for k in range(2):
                line = jnp.broadcast_to(taps_all[z, pl.ds(32 * k + b, 1)], (112, 128))
                parts.append(pltpu.roll(line, 0, 1, stride=1, stride_axis=0))
            real, imag = parts
            low, high = pl.ds(pl.multiple_of(256 * b, 256), 128), pl.ds(pl.multiple_of(256 * b + 128, 128), 128)
            band[0, :, low] = real.astype(jnp.bfloat16)
            band[0, :, high] = (-imag).astype(jnp.bfloat16)
            band[1, :, low] = imag.astype(jnp.bfloat16)
            band[1, :, high] = real.astype(jnp.bfloat16)

        tiles = tiles_of(total)
        parts = [(at, size, n) for at, size in tiles for n in range(2 * cols // 256)]
        for group in range(width // 5):
            ahead = list(chunks) if group + 1 < width // 5 else []
            share = -(-len(ahead) // len(parts))
            for at, size, n in parts:
                for chunk in ahead[:share]:
                    build(group + 1, chunk)
                ahead = ahead[share:]
                deep = slice(1280 * group, 1280 * group + 1280)
                across = slice(256 * n, 256 * n + 256)
                lhs = jnp.concatenate([band[0, :size, deep], band[1, :size, deep]], 0)
                rhs = patches[group % 2][:, at : at + 128, across].reshape(1280, 256)
                product = jnp.dot(lhs, rhs, preferred_element_type=jnp.float32)
                rows_at = slice(2 * at, 2 * at + 2 * size)
                if group == 0:
                    conv_ref[rows_at, across] = product
                else:
                    conv_ref[rows_at, across] += product

        for at, size in tiles:
            total_ref = conv_ref.at[pl.ds(2 * at, 2 * size)]
            if z == 0 and at == 0:
                for copy in slow_copies:
                    copy.wait()
            phase = slow_all[z, margin + shift + at : margin + shift + at + size].astype(jnp.int32).astype(jnp.float32) * freq
            sine, cosine = sine_cosine(phase)
            line = lax.broadcasted_iota(jnp.int32, (size, cols), 0) + (me * rows - margin + shift + at)
            inside = (line >= 0) & (line < cells)
            kept = []
            for w in range(2):
                real = total_ref[:size, cols * w : cols * w + cols]
                imag = total_ref[size:, cols * w : cols * w + cols]
                for c, value in enumerate((real * cosine - imag * sine, real * sine + imag * cosine)):
                    value = jnp.where(inside, value, 0.0).astype(jnp.bfloat16)
                    kept.append(value.astype(jnp.float32))
                    if z + 1 < count:
                        target[w, c, at : at + size, :cols] = value
            corr[at : at + size] = (kept[0] * kept[2] + kept[1] * kept[3]) * factor
        image[z] = corr[margin - shift : margin - shift + rows].astype(image.dtype)

        @pl.when((me != freq_at) | (z != me))
        def _():
            outgoing(z).start()

    own = pltpu.make_async_copy(image.at[me], slots.at[freq_at], local.at[2])

    @pl.when(me == freq_at)
    def _():
        own.start()
        own.wait()

    for k in range(count):
        @pl.when((me != freq_at) | (k != freq_at))
        def _():
            incoming(k).wait_recv()
    result = slots[0].astype(jnp.float32)
    for k in range(1, count):
        result = result + slots[k].astype(jnp.float32)
    out_ref[0] = result
    for k in range(count):
        @pl.when((me != freq_at) | (k != me))
        def _():
            outgoing(k).wait_send()


def march(freq, surface, slow, taps, depth_count, rows, reach, factor):
    cols = surface.shape[4]
    width = 2 * reach + 1
    frame = rows + 4 * depth_count * reach
    peers = depth_count - 1
    return pl.pallas_call(
        functools.partial(march_kernel, depth_count, rows, reach, factor),
        out_shape=jax.ShapeDtypeStruct((1, rows, cols), jnp.float32),
        in_specs=[pl.BlockSpec(memory_space=pltpu.SMEM), pl.BlockSpec(memory_space=pl.ANY), VMEM, VMEM],
        out_specs=VMEM,
        scratch_shapes=[
            pltpu.VMEM((2, 2, frame, cols + 128), jnp.bfloat16),
            pltpu.VMEM((2, 2, frame, cols + 128), jnp.bfloat16),
            pltpu.VMEM((2, 112, 256 * width), jnp.bfloat16),
            pltpu.VMEM((10, 208, 2 * cols), jnp.bfloat16),
            pltpu.VMEM((10, 208, 2 * cols), jnp.bfloat16),
            pltpu.VMEM((384, 2 * cols), jnp.float32),
            pltpu.VMEM((192, cols), jnp.float32),
            pltpu.VMEM((depth_count, frame, cols), slow.dtype),
            pltpu.VMEM((depth_count,) + taps.shape, taps.dtype),
            pltpu.VMEM((depth_count, rows, cols), jnp.bfloat16),
            pltpu.VMEM((depth_count, rows, cols), jnp.bfloat16),
            pltpu.SemaphoreType.DMA((2, 2)),
            pltpu.SemaphoreType.DMA((3,)),
            pltpu.SemaphoreType.DMA((2, peers)),
            pltpu.SemaphoreType.DMA((2, peers)),
            pltpu.SemaphoreType.DMA((depth_count,)),
            pltpu.SemaphoreType.DMA((depth_count,)),
        ],
        compiler_params=pltpu.CompilerParams(collective_id=0, has_side_effects=True, vmem_limit_bytes=48 << 20),
    )(freq, surface, slow, taps)


def on_device_fused(surface, kernels, slowness, freq_index):
    depth_count = lax.axis_size("depth")
    rows = surface.shape[3] // depth_count
    width = kernels.shape[-1]
    reach = (width - 1) // 2
    taps = jnp.pad(jnp.swapaxes(kernels[0, 0], 1, 2), ((0, 0), (0, 32 - width), (0, 128 - width)))
    taps = taps.reshape(64, 128).astype(jnp.float32)
    slow = jnp.round(slowness[0] * SCALE).astype(jnp.int16)
    factor = 1.0 / math.sqrt(lax.axis_size("freq"))
    return march(freq_index, surface, slow, taps, depth_count, rows, reach, factor)


def fits(mesh):
    return mesh.shape["depth"] == 4 and mesh.shape["freq"] == 4


def solution(mesh):
    in_specs = (
        P("shots", "freq", None, None, None),
        P("depth", "freq", None, None, None),
        P("depth", None, None),
        P("freq"),
    )
    out_specs = P(("shots", "depth"), "freq", None)
    body = on_device_fused if fits(mesh) else on_device_general
    return jax.shard_map(
        body, mesh=mesh, in_specs=in_specs, out_specs=out_specs, check_vma=False
    )
```

```python
import functools
import math

import jax
import jax.numpy as jnp
from jax import lax
from jax.experimental import pallas as pl
from jax.experimental.pallas import tpu as pltpu
from jax.sharding import PartitionSpec as P


def with_halo(shard, sides, width):
    for axis, dim in sides:
        size, length = (lax.axis_size(axis), shard.shape[dim])
        up = [(i, (i + 1) % size) for i in range(size - 1)]
        down = [(j, i) for i, j in up]
        last = lax.slice_in_dim(shard, length - width, length, axis=dim)
        leading = lax.slice_in_dim(shard, 0, width, axis=dim)
        before = lax.ppermute(last, axis, up)
        after = lax.ppermute(leading, axis, down)
        shard = jnp.concatenate([before, shard, after], axis=dim)
    return shard


def convolve(padded, stencil, margin):
    rows_in = padded.shape[3]
    cells_y = padded.shape[4]
    tap_count = stencil.shape[-1]
    rows_out = rows_in - 2 * margin
    real_part = stencil[:, 0].astype(jnp.float32)
    imag_part = stencil[:, 1].astype(jnp.float32)
    filters = jnp.stack(
        [jnp.stack([real_part, -imag_part], 1), jnp.stack([imag_part, real_part], 1)], 1
    )
    offsets = lax.iota(jnp.int32, rows_in)[None, :] - lax.iota(jnp.int32, rows_out)[:, None]
    select = (offsets[None] == lax.iota(jnp.int32, tap_count)[:, None, None]).astype(jnp.float32)
    banded = jnp.einsum("fdcab,axk->fdxbck", filters, select).astype(jnp.bfloat16)
    widened = jnp.pad(padded, ((0, 0), (0, 0), (0, 0), (0, 0), (margin, margin)))
    patches = jnp.stack(
        [widened[:, :, :, :, shift : shift + cells_y] for shift in range(tap_count)], 0
    )
    return jnp.einsum("bwfcky,fdxbck->wfdxy", patches, banded, preferred_element_type=jnp.float32)


def rotate(convolved, phase_rate, freq_bins):
    phases = freq_bins[:, None, None] * phase_rate[None]
    cosines = jnp.cos(phases)
    sine_terms = jnp.sin(phases)
    real_out = convolved[:, :, 0] * cosines - convolved[:, :, 1] * sine_terms
    imag_out = convolved[:, :, 0] * sine_terms + convolved[:, :, 1] * cosines
    return jnp.stack([real_out, imag_out], 2).astype(jnp.bfloat16)


def correlate(stepped):
    widened = stepped.astype(jnp.float32)
    return jnp.sum(
        widened[0, :, 0] * widened[1, :, 0] + widened[0, :, 1] * widened[1, :, 1], axis=0
    )


def on_device_general(surface, kernels, slowness, freq_index):
    depth_count = lax.axis_size("depth")
    position = lax.axis_index("depth")
    cells_x = surface.shape[3]
    row_count = cells_x // depth_count
    tap_count = kernels.shape[-1]
    margin = (tap_count - 1) // 2
    start_row = position * row_count
    wavefield = lax.dynamic_slice_in_dim(surface, start_row, row_count, 3)
    stencils = lax.all_gather(kernels, "depth", axis=0, tiled=True)
    phase_rates = lax.all_to_all(slowness, "depth", split_axis=1, concat_axis=0, tiled=True)
    freq_bins = freq_index.astype(jnp.float32)

    def advance(wave, operands):
        stencil, phase_rate = operands
        padded = with_halo(wave, (("depth", 3),), margin)
        stepped = rotate(convolve(padded, stencil, margin), phase_rate, freq_bins)
        return (stepped, correlate(stepped))

    final_wave, partials = lax.scan(advance, wavefield, (stencils, phase_rates))
    moved = lax.all_to_all(partials, "depth", split_axis=0, concat_axis=1, tiled=True)
    summed = lax.psum_scatter(moved, "freq", scatter_dimension=1, tiled=True)
    return summed * (1.0 / math.sqrt(surface.shape[1] * lax.axis_size("freq")))


MESH = pl.DeviceIdType.MESH
VMEM = pl.BlockSpec(memory_space=pltpu.VMEM)
SCALE = 32767.0 / 0.02


def window(position, rows, cells, margin):
    length = min(cells, rows + 2 * margin)
    start = jnp.clip(position * rows - margin, 0, cells - length)
    offset = start - position * rows + 2 * margin
    return pl.multiple_of(start, 16), pl.multiple_of(offset, 16), length


def sine_cosine(phase):
    quarter = phase * 0.25
    sq = quarter * quarter
    sine = quarter * (1.0 + sq * (-1 / 6 + sq * (1 / 120 + sq * (-1 / 5040 + sq * (1 / 362880 - sq * (1 / 39916800))))))
    cosine = 1.0 + sq * (-0.5 + sq * (1 / 24 + sq * (-1 / 720 + sq * (1 / 40320 - sq * (1 / 3628800)))))
    for _ in range(2):
        sine, cosine = 2.0 * sine * cosine, 1.0 - 2.0 * sine * sine
    return sine, cosine


def tiles_of(total):
    if total <= 96:
        return [(0, total)]
    first = total // 2 // 16 * 16
    return [(0, first), (first, -(-(total - first) // 16) * 16)]


def march_kernel(depth_count, rows, reach, factor, freq_ref, surface_ref, slow_ref, taps_ref, out_ref,
                 wave0, wave1, band, even, odd, conv_ref, corr, slow_all, taps_all, image, slots,
                 sems, local, send, recv, image_send, image_recv):
    me = lax.axis_index("depth")
    freq_at = lax.axis_index("freq")
    count = depth_count
    margin = depth_count * reach
    cells = surface_ref.shape[3]
    cols = surface_ref.shape[4]
    width = 2 * reach + 1
    waves = (wave0, wave1)
    patches = (even, odd)

    barrier = pltpu.get_barrier_semaphore()
    for step in range(1, count):
        other = lax.rem(me + step, count)
        pl.semaphore_signal(barrier, inc=1, device_id={"depth": other}, device_id_type=MESH)
    for k in range(count):
        @pl.when((me != freq_at) | (k != freq_at))
        def _():
            pl.semaphore_signal(barrier, inc=1, device_id={"depth": freq_at, "freq": k}, device_id_type=MESH)
    pl.semaphore_wait(barrier, 2 * count - 1 - (me == freq_at).astype(jnp.int32))

    tap_copies = []
    slow_copies = []
    for step in range(1, count):
        other = lax.rem(me + step, count)
        start, offset, length = window(other, rows, cells, margin)
        tap_copies.append(pltpu.make_async_remote_copy(
            src_ref=taps_ref, dst_ref=taps_all.at[me],
            send_sem=send.at[0, step - 1], recv_sem=recv.at[0, step - 1],
            device_id={"depth": other}, device_id_type=MESH))
        slow_copies.append(pltpu.make_async_remote_copy(
            src_ref=slow_ref.at[pl.ds(start, length)],
            dst_ref=slow_all.at[me, pl.ds(offset, length)],
            send_sem=send.at[1, step - 1], recv_sem=recv.at[1, step - 1],
            device_id={"depth": other}, device_id_type=MESH))
    start, offset, length = window(me, rows, cells, margin)
    tap_copies.append(pltpu.make_async_copy(taps_ref, taps_all.at[me], local.at[0]))
    slow_copies.append(pltpu.make_async_copy(
        slow_ref.at[pl.ds(start, length)], slow_all.at[me, pl.ds(offset, length)], local.at[1]))
    for copy in tap_copies + slow_copies:
        copy.start()

    wave0[...] = jnp.zeros_like(wave0)
    copies = [
        pltpu.make_async_copy(
            surface_ref.at[w, 0, c, pl.ds(start, length)],
            wave0.at[w, c, pl.ds(offset, length), pl.ds(0, cols)],
            sems.at[w, c])
        for w in range(2) for c in range(2)
    ]
    for copy in copies:
        copy.start()
    wave1[:, :, :, cols:] = jnp.zeros(wave1.shape[:3] + (128,), wave1.dtype)
    top = rows + 2 * margin
    for held in patches:
        held[:, top:] = jnp.zeros((10, held.shape[1] - top, 2 * cols), held.dtype)
    for copy in copies:
        copy.wait()

    freq = freq_ref[0].astype(jnp.float32) * (1.0 / SCALE)

    def outgoing(z):
        return pltpu.make_async_remote_copy(
            src_ref=image.at[z], dst_ref=slots.at[freq_at],
            send_sem=image_send.at[z], recv_sem=image_recv.at[freq_at],
            device_id={"depth": z, "freq": me}, device_id_type=MESH)

    def incoming(k):
        return pltpu.make_async_remote_copy(
            src_ref=image.at[k], dst_ref=slots.at[k],
            send_sem=image_send.at[k], recv_sem=image_recv.at[k],
            device_id={"depth": k, "freq": me}, device_id_type=MESH)

    for z in range(count):
        source, target = waves[z % 2], waves[(z + 1) % 2]
        base = margin if z == 0 else 0
        shift = reach * (z + 1)
        total = rows + 2 * reach * (count - 1 - z)
        needed = -(-(total + 2 * reach) // 16) * 16

        def build(group, chunk):
            held = patches[group % 2]
            c, w, low = chunk
            size = min(64, needed - low)
            block = source[w, c, base + low : base + low + size]
            for b in range(5):
                moved = pltpu.roll(block, (reach - 5 * group - b) % (cols + 128), 1)
                held[2 * b + c, low : low + size, cols * w : cols * w + cols] = moved[:, :cols]

        chunks = [(c, w, low) for c in range(2) for w in range(2) for low in range(0, needed, 64)]
        for chunk in chunks:
            build(0, chunk)

        if z == 0:
            for copy in tap_copies:
                copy.wait()

        @pl.loop(0, width, unroll=width)
        def _(b):
            parts = []
            for k in range(2):
                line = jnp.broadcast_to(taps_all[z, pl.ds(32 * k + b, 1)], (112, 128))
                parts.append(pltpu.roll(line, 0, 1, stride=1, stride_axis=0))
            real, imag = parts
            low, high = pl.ds(pl.multiple_of(256 * b, 256), 128), pl.ds(pl.multiple_of(256 * b + 128, 128), 128)
            band[0, :, low] = real.astype(jnp.bfloat16)
            band[0, :, high] = (-imag).astype(jnp.bfloat16)
            band[1, :, low] = imag.astype(jnp.bfloat16)
            band[1, :, high] = real.astype(jnp.bfloat16)

        tiles = tiles_of(total)
        parts = [(at, size, n) for at, size in tiles for n in range(2 * cols // 256)]
        for group in range(width // 5):
            ahead = list(chunks) if group + 1 < width // 5 else []
            share = -(-len(ahead) // len(parts))
            for at, size, n in parts:
                for chunk in ahead[:share]:
                    build(group + 1, chunk)
                ahead = ahead[share:]
                deep = slice(1280 * group, 1280 * group + 1280)
                across = slice(256 * n, 256 * n + 256)
                lhs = jnp.concatenate([band[0, :size, deep], band[1, :size, deep]], 0)
                rhs = patches[group % 2][:, at : at + 128, across].reshape(1280, 256)
                product = jnp.dot(lhs, rhs, preferred_element_type=jnp.float32)
                rows_at = slice(2 * at, 2 * at + 2 * size)
                if group == 0:
                    conv_ref[rows_at, across] = product
                else:
                    conv_ref[rows_at, across] += product

        for at, size in tiles:
            total_ref = conv_ref.at[pl.ds(2 * at, 2 * size)]
            if z == 0 and at == 0:
                for copy in slow_copies:
                    copy.wait()
            phase = slow_all[z, margin + shift + at : margin + shift + at + size].astype(jnp.int32).astype(jnp.float32) * freq
            sine, cosine = sine_cosine(phase)
            line = lax.broadcasted_iota(jnp.int32, (size, cols), 0) + (me * rows - margin + shift + at)
            inside = (line >= 0) & (line < cells)
            kept = []
            for w in range(2):
                real = total_ref[:size, cols * w : cols * w + cols]
                imag = total_ref[size:, cols * w : cols * w + cols]
                for c, value in enumerate((real * cosine - imag * sine, real * sine + imag * cosine)):
                    value = jnp.where(inside, value, 0.0).astype(jnp.bfloat16)
                    kept.append(value.astype(jnp.float32))
                    if z + 1 < count:
                        target[w, c, at : at + size, :cols] = value
            corr[at : at + size] = (kept[0] * kept[2] + kept[1] * kept[3]) * factor
        image[z] = corr[margin - shift : margin - shift + rows].astype(image.dtype)

        @pl.when((me != freq_at) | (z != me))
        def _():
            outgoing(z).start()

    own = pltpu.make_async_copy(image.at[me], slots.at[freq_at], local.at[2])

    @pl.when(me == freq_at)
    def _():
        own.start()
        own.wait()

    for k in range(count):
        @pl.when((me != freq_at) | (k != freq_at))
        def _():
            incoming(k).wait_recv()
    result = slots[0].astype(jnp.float32)
    for k in range(1, count):
        result = result + slots[k].astype(jnp.float32)
    out_ref[0] = result
    for k in range(count):
        @pl.when((me != freq_at) | (k != me))
        def _():
            outgoing(k).wait_send()


def march(freq, surface, slow, taps, depth_count, rows, reach, factor):
    cols = surface.shape[4]
    width = 2 * reach + 1
    frame = rows + 4 * depth_count * reach
    peers = depth_count - 1
    return pl.pallas_call(
        functools.partial(march_kernel, depth_count, rows, reach, factor),
        out_shape=jax.ShapeDtypeStruct((1, rows, cols), jnp.float32),
        in_specs=[pl.BlockSpec(memory_space=pltpu.SMEM), pl.BlockSpec(memory_space=pl.ANY), VMEM, VMEM],
        out_specs=VMEM,
        scratch_shapes=[
            pltpu.VMEM((2, 2, frame, cols + 128), jnp.bfloat16),
            pltpu.VMEM((2, 2, frame, cols + 128), jnp.bfloat16),
            pltpu.VMEM((2, 112, 256 * width), jnp.bfloat16),
            pltpu.VMEM((10, 208, 2 * cols), jnp.bfloat16),
            pltpu.VMEM((10, 208, 2 * cols), jnp.bfloat16),
            pltpu.VMEM((384, 2 * cols), jnp.float32),
            pltpu.VMEM((192, cols), jnp.float32),
            pltpu.VMEM((depth_count, frame, cols), slow.dtype),
            pltpu.VMEM((depth_count,) + taps.shape, taps.dtype),
            pltpu.VMEM((depth_count, rows, cols), jnp.bfloat16),
            pltpu.VMEM((depth_count, rows, cols), jnp.bfloat16),
            pltpu.SemaphoreType.DMA((2, 2)),
            pltpu.SemaphoreType.DMA((3,)),
            pltpu.SemaphoreType.DMA((2, peers)),
            pltpu.SemaphoreType.DMA((2, peers)),
            pltpu.SemaphoreType.DMA((depth_count,)),
            pltpu.SemaphoreType.DMA((depth_count,)),
        ],
        compiler_params=pltpu.CompilerParams(collective_id=0, has_side_effects=True, vmem_limit_bytes=48 << 20),
    )(freq, surface, slow, taps)


def on_device_fused(surface, kernels, slowness, freq_index):
    depth_count = lax.axis_size("depth")
    rows = surface.shape[3] // depth_count
    width = kernels.shape[-1]
    reach = (width - 1) // 2
    taps = jnp.pad(jnp.swapaxes(kernels[0, 0], 1, 2), ((0, 0), (0, 32 - width), (0, 128 - width)))
    taps = taps.reshape(64, 128).astype(jnp.float32)
    slow = jnp.round(slowness[0] * SCALE).astype(jnp.int16)
    factor = 1.0 / math.sqrt(lax.axis_size("freq"))
    return march(freq_index, surface, slow, taps, depth_count, rows, reach, factor)


def fits(mesh):
    return mesh.shape["depth"] == 4 and mesh.shape["freq"] == 4


def solution(mesh):
    in_specs = (
        P("shots", "freq", None, None, None),
        P("depth", "freq", None, None, None),
        P("depth", None, None),
        P("freq"),
    )
    out_specs = P(("shots", "depth"), "freq", None)
    body = on_device_fused if fits(mesh) else on_device_general
    return jax.shard_map(
        body, mesh=mesh, in_specs=in_specs, out_specs=out_specs, check_vma=False
    )
```
